128 devices in a mesh: fit: 16 (over z, x), basis: 4 (over y_hi, core), occ: 2 (over y_lo).
Axes of the slice: x: 4, y: 4 (y_hi: 2, y_lo: 2; y = y_hi * 2 + y_lo), z: 4, core: 2. Of those that a mesh axis runs over, the one named last changes fastest.
Arguments:
- ints: bfloat16 [256, 12288, 128], P('fit', 'basis'), may hold values from -0.5 to 0.5
- coeffs: bfloat16 [12288, 128], P('fit', 'occ'), may hold values from -0.59765625 to 0.59765625
- offsets: int32 [192, 2], P('basis'), may hold values from 0 to 191
- mask: int32 [192, 2], P('basis'), may hold values 0 or 1
Outputs:
- exchange: float32 [12288, 4, 512], P(('fit', 'occ'), None, 'basis')
The draws below stay inside these ranges and needn't reach their ends.
All inputs are finite; a program needn't handle non-finite values. No bound on the sum of `mask` on one device may be relied on, other than what follows from the above.
Results may differ from the reference program's by a relative error of at most 0.003.
Values may be sent and summed in bfloat16 or wider, within the bound.
A program may use at most 192 MiB of HBM per device.

```python
import jax
import jax.numpy as jnp
import numpy as np
from jax import lax

NB = 12288
BLK = 64
NNZ = 2
MU_DEV = 128
NAUX = 256
NOCC = 32
N_BASIS = 4


def with_ends(array, stream_key, low, high):
    longest = array.shape.index(max(array.shape))
    spots = []
    for shift in (0, 1):
        where = [jax.random.randint(jax.random.fold_in(stream_key, axis), (), 0, length) for axis, length in enumerate(array.shape)]
        where[longest] = (where[longest] + shift) % array.shape[longest]
        spots.append(tuple(where))
    return array.at[spots[0]].set(low).at[spots[1]].set(high)


def levels(stream_key, extent, cuts, smallest, largest):
    level = 1.0
    for dim, parts in cuts:
        heights = jax.random.uniform(jax.random.fold_in(jax.random.fold_in(stream_key, 6), dim), (parts,), jnp.float32, smallest / len(cuts), largest / len(cuts))
        level = level * jnp.repeat(jnp.exp(heights), extent[dim] // parts).reshape((-1,) + (1,) * (len(extent) - 1 - dim))
    return level


def noise(own_key, shape, scale, limit, shards=(), kind=jnp.bfloat16):
    gain = levels(own_key, shape, shards, -0.22, 0.18) if shards else 1.0
    result = jax.random.normal(own_key, shape, jnp.float32) * scale * gain
    return jnp.minimum(jnp.maximum(result, -limit), limit).astype(kind)


def setup_inputs(seed: int = 0) -> dict:
    streams_of = jax.random.split(jax.random.key(seed), 5)
    return {
        "ints": noise(streams_of[0], (NAUX, NB, NNZ * BLK), (NNZ * BLK) ** -0.5, 0.5, ((0, 16), (1, 4))),
        "coeffs": noise(streams_of[1], (NB, 4 * NOCC), 0.1, 0.59765625, ((0, 16), (1, 2))),
        "offsets": with_ends(jax.random.randint(streams_of[2], (NB // BLK, NNZ), 0, NB // BLK), jax.random.fold_in(streams_of[2], 1), 0, (NB // BLK) - 1).astype(jnp.int32),
        "mask": with_ends((jax.random.randint(streams_of[3], (NB // BLK, NNZ), 0, 4) < 3).astype(jnp.int32), jax.random.fold_in(streams_of[3], 1), 0, 1),
    }


SIGN_ENTRIES = ((0, 0, 0, 1), (0, 1, 1, 1), (0, 2, 2, 1), (0, 3, 3, 1),
                (1, 0, 1, -1), (1, 1, 0, 1), (1, 2, 3, -1), (1, 3, 2, 1),
                (2, 0, 2, -1), (2, 1, 3, 1), (2, 2, 0, 1), (2, 3, 1, -1),
                (3, 0, 3, -1), (3, 1, 2, -1), (3, 2, 1, 1), (3, 3, 0, 1))


def sign_table():
    table = np.zeros((4, 4, 4), np.float32)
    for entry in SIGN_ENTRIES:
        table[entry[0], entry[1], entry[2]] = entry[3]
    return table


def reference(ints, coeffs, offsets, mask):
    rows_dev = NB // N_BASIS
    blocks = coeffs.reshape(NB // BLK, BLK, -1)
    picked = jnp.take(blocks, offsets, axis=0) * mask[:, :, None, None].astype(jnp.bfloat16)
    picked = picked.reshape(NB // BLK, NNZ * BLK, -1).astype(jnp.float32)
    index = jnp.arange(MU_DEV * N_BASIS, dtype=jnp.int32)
    chosen = ((index // MU_DEV) * rows_dev + index % MU_DEV).astype(jnp.int32)
    count = MU_DEV * N_BASIS
    sign = jnp.asarray(sign_table(), jnp.float32)

    def advance(total, slab):
        grouped = slab.astype(jnp.float32).reshape(NB // BLK, BLK, NNZ * BLK)
        half = jnp.einsum("rjk,rkw->rjw", grouped, picked).reshape(NB, -1).astype(jnp.bfloat16)
        window = jnp.take(half, chosen, axis=0).astype(jnp.float32).reshape(count, -1, 4)
        mixed = jnp.einsum("rqs,mkq->rmks", sign, window).reshape(4 * count, -1).astype(jnp.bfloat16)
        term = lax.dot_general(half, mixed, (((1,), (1,)), ((), ())), preferred_element_type=jnp.float32)
        return total + term, None

    total, unused = lax.scan(advance, jnp.zeros((NB, 4 * count), jnp.float32), ints)
    return total.reshape(NB, 4, count)
```

```python
import jax
import jax.numpy as jnp
import numpy as np
from jax import lax
from jax.sharding import PartitionSpec as P

BLK = 64
NNZ = 2
MU_DEV = 128
SIGN_ENTRIES = (
    (0, 0, 0, 1),
    (0, 1, 1, 1),
    (0, 2, 2, 1),
    (0, 3, 3, 1),
    (1, 0, 1, -1),
    (1, 1, 0, 1),
    (1, 2, 3, -1),
    (1, 3, 2, 1),
    (2, 0, 2, -1),
    (2, 1, 3, 1),
    (2, 2, 0, 1),
    (2, 3, 1, -1),
    (3, 0, 3, -1),
    (3, 1, 2, -1),
    (3, 2, 1, 1),
    (3, 3, 0, 1),
)


def signed_permutations(width):
    table = np.zeros((4, width, width), np.float32)
    for r, q, s, sign in SIGN_ENTRIES:
        for i in range(width // 4):
            table[r, 4 * i + q, 4 * i + s] = sign
    return table


def half_rows(ints, picked):
    out = jnp.einsum("arjk,rkw->rjaw", ints, picked, preferred_element_type=jnp.float32)
    rows = out.shape[0] * out.shape[1]
    return out.astype(jnp.bfloat16).reshape(rows, -1)


def shards(ints, coeffs, offsets, mask):
    occ = lax.axis_index("occ")
    gathered = lax.all_gather(coeffs, ("fit", "occ"), axis=0)
    gathered = gathered.reshape(16, 2, *coeffs.shape)
    full = jnp.moveaxis(gathered, 1, 2).reshape(-1, 2 * coeffs.shape[1])
    width = full.shape[1]
    blocks = full.reshape(-1, BLK, width)
    aux, rows, stored = ints.shape
    chunk = rows // 8
    per = chunk // BLK

    def picks(off, msk):
        got = jnp.take(blocks, off, axis=0) * msk[:, :, None, None].astype(jnp.bfloat16)
        return got.reshape(off.shape[0], NNZ * BLK, width)

    nwin = MU_DEV // BLK
    window = half_rows(
        ints[:, :MU_DEV].reshape(aux, nwin, BLK, stored), picks(offsets[:nwin], mask[:nwin])
    )
    windows = lax.all_gather(window, "basis", axis=0, tiled=True)
    table = jnp.asarray(signed_permutations(width), jnp.bfloat16)
    mixed = jnp.einsum(
        "bmak,rks->brmas",
        windows.reshape(4, MU_DEV, aux, width),
        table,
        preferred_element_type=jnp.float32,
    ).astype(jnp.bfloat16)
    mixed = mixed.reshape(4, 4 * MU_DEV, aux * width)

    mine = lax.dynamic_index_in_dim(ints.reshape(aux, 4, 2, chunk, stored), occ, 2, False)
    off = lax.dynamic_index_in_dim(offsets.reshape(4, 2, per, NNZ), occ, 1, False)
    msk = lax.dynamic_index_in_dim(mask.reshape(4, 2, per, NNZ), occ, 1, False)
    half = half_rows(
        mine.reshape(aux, 4 * per, BLK, stored),
        picks(off.reshape(4 * per, NNZ), msk.reshape(4 * per, NNZ)),
    )
    terms = jnp.stack(
        [
            lax.dot_general(
                half, mixed[b], (((1,), (1,)), ((), ())), preferred_element_type=jnp.float32
            )
            for b in range(4)
        ]
    )
    terms = terms.reshape(16 * chunk, 4 * MU_DEV)
    summed = lax.psum_scatter(terms, "fit", scatter_dimension=0, tiled=True)
    moves = []
    for z in range(4):
        for x in range(4):
            for b in range(4):
                moves.append(((z * 4 + x) * 4 + b, (b * 4 + x) * 4 + z))
    result = lax.ppermute(summed, ("fit", "basis"), moves)
    return result.reshape(chunk, 4, MU_DEV)


def solution(mesh):
    return jax.shard_map(
        shards,
        mesh=mesh,
        in_specs=(P("fit", "basis", None), P("fit", "occ"), P("basis", None), P("basis", None)),
        out_specs=P(("fit", "occ"), None, "basis"),
        check_vma=False,
    )
```

```python
import functools

import jax
import jax.numpy as jnp
import numpy as np
from jax import lax
from jax.experimental import pallas as pl
from jax.experimental.pallas import tpu as pltpu
from jax.sharding import PartitionSpec as P

BLK = 64
NNZ = 2
MU_DEV = 128
AUX = 16
ROWS = 3072
CHUNK = 384
QUART = 96
WIDTH = 128
KDIM = AUX * WIDTH
MESH = pl.DeviceIdType.MESH
SIGN_ENTRIES = (
    (0, 0, 0, 1),
    (0, 1, 1, 1),
    (0, 2, 2, 1),
    (0, 3, 3, 1),
    (1, 0, 1, -1),
    (1, 1, 0, 1),
    (1, 2, 3, -1),
    (1, 3, 2, 1),
    (2, 0, 2, -1),
    (2, 1, 3, 1),
    (2, 2, 0, 1),
    (2, 3, 1, -1),
    (3, 0, 3, -1),
    (3, 1, 2, -1),
    (3, 2, 1, 1),
    (3, 3, 0, 1),
)


def signed_permutations():
    table = np.zeros((WIDTH, 4, WIDTH), np.float32)
    for r, q, s, sign in SIGN_ENTRIES:
        for i in range(WIDTH // 4):
            table[4 * i + q, r, 4 * i + s] = sign
    return table.reshape(WIDTH, 4 * WIDTH)


def dot_nt(a, b):
    return lax.dot_general(
        a, b, (((1,), (1,)), ((), ())), preferred_element_type=jnp.float32
    )


def kernel(
    ints, coef, table, offs, mask, out,
    win_in, ints_v, G, win, mixed, half, part,
    r1a, r1b, r2a, r2b, q1, q2, fin,
    lsem, gs, gr, ws, wr, s1s, s1r, s2s, s2r, ts, tr,
):
    fit = lax.axis_index("fit")
    b = lax.axis_index("basis")
    yl = lax.axis_index("occ")
    z = fit // 4
    x = fit % 4
    yh = b // 2
    c = b % 2
    oyl = 1 - yl
    partner = 2 * yh + (1 - c)

    def basis_at(k):
        return 2 * ((yh + k // 2) % 2) + (c + k % 2) % 2

    def dev(zz, xx, bb, ll):
        return (zz * 4 + xx, bb, ll)

    def rows(q):
        return pl.ds(pl.multiple_of(q * QUART, QUART), QUART)

    locals_ = [pltpu.make_async_copy(ints.at[:, pl.ds(0, MU_DEV), :], win_in, lsem.at[0])]
    for xx in range(4):
        start = pl.multiple_of((2 * xx + yl) * CHUNK, CHUNK)
        locals_.append(
            pltpu.make_async_copy(
                ints.at[:, pl.ds(start, CHUNK), :], ints_v.at[xx], lsem.at[1 + xx]
            )
        )
    for copy in locals_:
        copy.start()

    for t in range(3):
        G[z, x, yl, c, t] = coef[:, pl.ds(pl.multiple_of(c * CHUNK + t * 128, 128), 128)]

    barrier = pltpu.get_barrier_semaphore()

    def greet(target):
        pl.semaphore_signal(barrier, inc=1, device_id=target, device_id_type=MESH)

    for dz in range(4):
        for k in range(4):
            if dz or k:
                greet(dev((z + dz) % 4, x, basis_at(k), yl))
    for d in (1, 2, 3):
        greet(dev(z, (x + d) % 4, b, yl))
    greet(dev(z, x, b, oyl))
    greet(dev(z, x, basis_at(2), oyl))
    pl.semaphore_wait(barrier, 20)

    def send(src, dst, ssem, rsem, target):
        copy = pltpu.make_async_remote_copy(
            src_ref=src,
            dst_ref=dst,
            send_sem=ssem,
            recv_sem=rsem,
            device_id=target,
            device_id_type=MESH,
        )
        copy.start()
        return copy

    sent = []


    def gather(src, dst, n, target):
        copy = send(src, dst, gs.at[n], gr.at[n], target)
        sent.append(copy)
        return copy

    mine = G.at[z, x, yl, c]
    first = gather(mine, mine, 0, dev(z, x, b, oyl))
    first.wait_recv()
    along_x = []
    along_z = []
    ga = G.at[z, x, 0, c]
    gb = G.at[z, x, 1, c]
    for d in (1, 3, 2):
        along_x.append(gather(ga, ga, d, dev(z, (x + d) % 4, b, yl)))
        along_z.append(gather(gb, gb, 3 + d, dev((z + d) % 4, x, b, yl)))
    for one, two in zip(along_x, along_z):
        one.wait_recv()
        two.wait_recv()
    zp, zm, z2 = (z + 1) % 4, (z + 3) % 4, (z + 2) % 4
    xp, xm, x2 = (x + 1) % 4, (x + 3) % 4, (x + 2) % 4
    onchip = []

    def group(color, at):
        return G.at[at, :, 0, c] if color == 0 else G.at[:, at, 1, c]

    def pair(color, at, n):
        ref = group(color, at)
        onchip.append(gather(ref, ref, n, dev(z, x, partner, yl)))

    up = (dev(zp, x, b, yl), dev(z, xp, b, yl))
    down = (dev(zm, x, b, yl), dev(z, xm, b, yl))
    here = (z, x)
    above = (zp, xp)
    below = (zm, xm)
    far = (z2, x2)
    ups, downs = [], []
    for color in range(2):
        ref = group(color, here[color])
        ups.append(gather(ref, ref, 7 + color, up[color]))
        downs.append(gather(ref, ref, 9 + color, down[color]))
    for color in range(2):
        pair(color, here[color], 15 + color)
    fars = []
    for color in range(2):
        ups[color].wait_recv()
        ref = group(color, below[color]).at[:, :, pl.ds(0, 32), :]
        fars.append(gather(ref, ref, 11 + color, up[color]))
        downs[color].wait_recv()
        ref = group(color, above[color]).at[:, :, pl.ds(32, 32), :]
        fars.append(gather(ref, ref, 13 + color, down[color]))
        pair(color, below[color], 17 + color)
        pair(color, above[color], 19 + color)
    for copy in fars:
        copy.wait_recv()
    for color in range(2):
        pair(color, far[color], 21 + color)
    for copy in onchip:
        copy.wait_recv()

    lane = lax.broadcasted_iota(jnp.int32, (WIDTH, WIDTH), 1)

    def picked(rb):
        sides = []
        for k in range(NNZ):
            off = offs[k, rb]
            keep = mask[k, rb].astype(jnp.float32)
            odd = lax.rem(off, 2).astype(jnp.float32) * keep
            even = keep - odd
            tile = lax.div(off, 2)
            f = lax.div(tile, 6)
            core = lax.div(lax.rem(tile, 6), 3)
            at = (lax.div(f, 4), lax.rem(f, 4))
            got = jnp.concatenate(
                [G[(*at, o, core, lax.rem(tile, 3))] for o in range(2)], axis=0
            ).astype(jnp.float32)
            turned = pltpu.roll(got, 64, 1)
            if k == 0:
                sides.append(got * even + turned * odd)
            else:
                sides.append(got * odd + turned * even)
        return jnp.where(lane < BLK, sides[0], sides[1]).astype(jnp.bfloat16)

    locals_[0].wait()
    for rb in range(MU_DEV // BLK):
        slab = win_in[:, rb * BLK : (rb + 1) * BLK, :].reshape(AUX * BLK, WIDTH)
        got = dot_nt(slab, picked(rb)).astype(jnp.bfloat16)
        for p in range(AUX):
            win[b, rb * BLK : (rb + 1) * BLK, p * WIDTH : (p + 1) * WIDTH] = got[
                p * BLK : (p + 1) * BLK
            ]
    window = [
        send(win.at[b], win.at[b], ws.at[0], wr.at[0], dev(z, x, partner, yl)),
        send(win.at[b], win.at[b], ws.at[1], wr.at[1], dev(z, x, basis_at(2), oyl)),
    ]
    sent.extend(window)

    for xx in range(4):
        locals_[1 + xx].wait()

    @pl.loop(0, 24)
    def _(i):
        xx = i // 6
        r = i % 6
        slab = ints_v[xx, :, pl.ds(pl.multiple_of(r * BLK, BLK), BLK), :]
        weights = picked((2 * xx + yl) * 6 + r)
        got = dot_nt(slab.reshape(AUX * BLK, WIDTH), weights).astype(jnp.bfloat16)
        at = pl.ds(pl.multiple_of(i * BLK, BLK), BLK)
        for p in range(AUX):
            half[at, p * WIDTH : (p + 1) * WIDTH] = got[p * BLK : (p + 1) * BLK]

    def dots(k):
        bb = basis_at(k)

        @pl.loop(0, AUX)
        def _(p):
            at = pl.ds(pl.multiple_of(p * WIDTH, WIDTH), WIDTH)
            got = jnp.dot(win[bb, :, at], table[...], preferred_element_type=jnp.float32)
            got = got.astype(jnp.bfloat16)
            for r in range(4):
                mixed[r // 2, (r % 2) * 128 : (r % 2) * 128 + 128, at] = got[
                    :, r * WIDTH : (r + 1) * WIDTH
                ]

        @pl.loop(0, 8)
        def _(i):
            h = i // 4
            xx = i % 4
            at = pl.ds(pl.multiple_of(xx * CHUNK, CHUNK), CHUNK)
            part[k, h, xx] = dot_nt(half[at, :], mixed[h]).astype(jnp.bfloat16)

    def chunk_at(k, h, stage, q):
        if k % 2 == 0:
            if stage == 0:
                return part.at[k, h, q]
            return part.at[k, h, x, rows(q)]
        if stage == 0:
            return part.at[k, h, :, rows(q)]
        return part.at[k, h, q, rows(z)]

    def recv_one(k, stage, side):
        if stage:
            return q1.at[k, side]
        return r1a.at[k // 2, side] if k % 2 == 0 else r1b.at[k // 2, side]

    def recv_two(k, stage, side, h):
        if stage:
            return q2.at[k, side, h]
        return r2a.at[k // 2, side, h] if k % 2 == 0 else r2b.at[k // 2, side, h]

    flights = {}

    def ring(k, stage):
        color = (k + stage) % 2
        if color == 0:
            return x, dev(z, xp, b, yl), dev(z, xm, b, yl)
        return z, dev(zp, x, b, yl), dev(zm, x, b, yl)

    def launch(k, stage):
        me, plus, minus = ring(k, stage)
        n = k * 2 + stage
        two = (me + 2) % 4
        nxt, prv = (me + 1) % 4, (me + 3) % 4
        got = {}
        for side, target in ((0, plus), (1, minus)):
            got["one", side] = send(
                chunk_at(k, side, stage, two), recv_one(k, stage, side),
                s1s.at[n, side], s1r.at[n, side], target,
            )
        got["two", 0, 1] = send(
            chunk_at(k, 1, stage, nxt), recv_two(k, stage, 0, 1),
            s2s.at[n, 0, 1], s2r.at[n, 0, 1], plus,
        )
        got["two", 1, 0] = send(
            chunk_at(k, 0, stage, prv), recv_two(k, stage, 1, 0),
            s2s.at[n, 1, 0], s2r.at[n, 1, 0], minus,
        )
        flights[k, stage] = got

    def relay(k, stage):
        me, plus, minus = ring(k, stage)
        n = k * 2 + stage
        got = flights[k, stage]
        for side, target in ((0, plus), (1, minus)):
            got["one", side].wait_recv()
            at = (me + 1) % 4 if side == 0 else (me + 3) % 4
            ref = chunk_at(k, side, stage, at)
            total = ref[...].astype(jnp.float32)
            total += recv_one(k, stage, side)[...].astype(jnp.float32)
            ref[...] = total.astype(jnp.bfloat16)
            got["two", side, side] = send(
                chunk_at(k, side, stage, at), recv_two(k, stage, side, side),
                s2s.at[n, side, side], s2r.at[n, side, side], target,
            )

    def collect(k, stage):
        me, plus, minus = ring(k, stage)
        got = flights[k, stage]
        for h in range(2):
            got["two", 0, h].wait_recv()
            got["two", 1, h].wait_recv()
            ref = chunk_at(k, h, stage, me)
            total = ref[...].astype(jnp.float32)
            total += recv_two(k, stage, 0, h)[...].astype(jnp.float32)
            total += recv_two(k, stage, 1, h)[...].astype(jnp.float32)
            if stage == 0:
                ref[...] = total.astype(jnp.bfloat16)
            else:
                fin[k, :, h * 256 : (h + 1) * 256] = total

    finals = []

    def deliver(k):
        target = dev(b, x, basis_at(k), yl)
        if k == 0:
            same = z == b

            @pl.when(same)
            def _():
                pltpu.make_async_copy(fin.at[k], out.at[z], tr.at[z]).start()

            @pl.when(jnp.logical_not(same))
            def _():
                send(fin.at[k], out.at[z], ts.at[k], tr.at[z], target)
        else:
            finals.append(send(fin.at[k], out.at[z], ts.at[k], tr.at[z], target))

    dots(0)
    launch(0, 0)
    window[0].wait_recv()
    dots(1)
    launch(1, 0)
    window[1].wait_recv()
    other = win.at[basis_at(2)]
    forward = send(other, other, ws.at[2], wr.at[2], dev(z, x, partner, yl))
    sent.append(forward)
    relay(0, 0)
    dots(2)
    launch(2, 0)
    relay(1, 0)
    forward.wait_recv()
    dots(3)
    launch(3, 0)
    collect(0, 0)
    launch(0, 1)
    relay(2, 0)
    collect(1, 0)
    launch(1, 1)
    relay(3, 0)
    relay(0, 1)
    relay(1, 1)
    collect(0, 1)
    deliver(0)
    collect(1, 1)
    deliver(1)
    collect(2, 0)
    launch(2, 1)
    collect(3, 0)
    launch(3, 1)
    relay(2, 1)
    relay(3, 1)
    collect(2, 1)
    deliver(2)
    collect(3, 1)
    deliver(3)

    for q in range(4):
        pltpu.make_async_copy(fin.at[0], out.at[q], tr.at[q]).wait()
    for copy in sent:
        copy.wait_send()
    for got in flights.values():
        for copy in got.values():
            copy.wait_send()

    @pl.when(z != b)
    def _():
        pltpu.make_async_remote_copy(
            src_ref=fin.at[0], dst_ref=out.at[z], send_sem=ts.at[0], recv_sem=tr.at[z],
            device_id=dev(b, x, b, yl), device_id_type=MESH,
        ).wait_send()

    for copy in finals:
        copy.wait_send()


def shards(ints, coeffs, offsets, mask):
    table = jnp.asarray(signed_permutations(), jnp.bfloat16)
    bf16, f32 = jnp.bfloat16, jnp.float32
    vmem = pl.BlockSpec(memory_space=pltpu.VMEM)
    smem = pl.BlockSpec(memory_space=pltpu.SMEM)
    dma = pltpu.SemaphoreType.DMA
    result = pl.pallas_call(
        kernel,
        out_shape=jax.ShapeDtypeStruct((4, QUART, 512), f32),
        in_specs=[pl.BlockSpec(memory_space=pl.ANY), vmem, vmem, smem, smem],
        out_specs=vmem,
        scratch_shapes=[
            pltpu.VMEM((AUX, MU_DEV, WIDTH), bf16),
            pltpu.VMEM((4, AUX, CHUNK, WIDTH), bf16),
            pltpu.VMEM((4, 4, 2, 2, 3, 64, 128), bf16),
            pltpu.VMEM((4, MU_DEV, KDIM), bf16),
            pltpu.VMEM((2, 256, KDIM), bf16),
            pltpu.VMEM((4 * CHUNK, KDIM), bf16),
            pltpu.VMEM((4, 2, 4, CHUNK, 256), bf16),
            pltpu.VMEM((2, 2, CHUNK, 256), bf16),
            pltpu.VMEM((2, 2, 4, QUART, 256), bf16),
            pltpu.VMEM((2, 2, 2, CHUNK, 256), bf16),
            pltpu.VMEM((2, 2, 2, 4, QUART, 256), bf16),
            pltpu.VMEM((4, 2, QUART, 256), bf16),
            pltpu.VMEM((4, 2, 2, QUART, 256), bf16),
            pltpu.VMEM((4, QUART, 512), f32),
            dma((5,)),
            dma((23,)),
            dma((23,)),
            dma((3,)),
            dma((3,)),
            dma((8, 2)),
            dma((8, 2)),
            dma((8, 2, 2)),
            dma((8, 2, 2)),
            dma((4,)),
            dma((4,)),
        ],
        compiler_params=pltpu.CompilerParams(
            collective_id=0, has_side_effects=True, vmem_limit_bytes=60 * 1024 * 1024
        ),
        name="exchange",
    )(ints, coeffs.T, table, offsets.T, mask.T)
    return result.reshape(CHUNK, 4, MU_DEV)


def solution(mesh):
    return jax.shard_map(
        shards,
        mesh=mesh,
        in_specs=(P("fit", "basis", None), P("fit", "occ"), P("basis", None), P("basis", None)),
        out_specs=P(("fit", "occ"), None, "basis"),
        check_vma=False,
    )
```

```python
import functools

import jax
import jax.numpy as jnp
import numpy as np
from jax import lax
from jax.experimental import pallas as pl
from jax.experimental.pallas import tpu as pltpu
from jax.sharding import PartitionSpec as P

BLK = 64
NNZ = 2
MU_DEV = 128
AUX = 16
ROWS = 3072
CHUNK = 384
QUART = 96
WIDTH = 128
KDIM = AUX * WIDTH
MESH = pl.DeviceIdType.MESH
SIGN_ENTRIES = (
    (0, 0, 0, 1),
    (0, 1, 1, 1),
    (0, 2, 2, 1),
    (0, 3, 3, 1),
    (1, 0, 1, -1),
    (1, 1, 0, 1),
    (1, 2, 3, -1),
    (1, 3, 2, 1),
    (2, 0, 2, -1),
    (2, 1, 3, 1),
    (2, 2, 0, 1),
    (2, 3, 1, -1),
    (3, 0, 3, -1),
    (3, 1, 2, -1),
    (3, 2, 1, 1),
    (3, 3, 0, 1),
)


def signed_permutations():
    table = np.zeros((WIDTH, 4, WIDTH), np.float32)
    for r, q, s, sign in SIGN_ENTRIES:
        for i in range(WIDTH // 4):
            table[4 * i + q, r, 4 * i + s] = sign
    return table.reshape(WIDTH, 4 * WIDTH)


def dot_nt(a, b):
    return lax.dot_general(
        a, b, (((1,), (1,)), ((), ())), preferred_element_type=jnp.float32
    )


def kernel(
    ints, coef, table, offs, mask, out,
    win_in, ints_v, G, win, mixed, half, part, partf,
    r1a, r1b, r2a, r2b, quarter, fin, last,
    lsem, gs, gr, ws, wr, s1s, s1r, s2s, s2r, qs, qr, ts, tr,
):
    fit = lax.axis_index("fit")
    b = lax.axis_index("basis")
    yl = lax.axis_index("occ")
    z = fit // 4
    x = fit % 4
    yh = b // 2
    c = b % 2
    oyl = 1 - yl
    partner = 2 * yh + (1 - c)

    def basis_at(k):
        return 2 * ((yh + k // 2) % 2) + (c + k % 2) % 2

    def dev(zz, xx, bb, ll):
        return (zz * 4 + xx, bb, ll)

    def rows(q):
        return pl.ds(pl.multiple_of(q * QUART, QUART), QUART)

    locals_ = [pltpu.make_async_copy(ints.at[:, pl.ds(0, MU_DEV), :], win_in, lsem.at[0])]
    for xx in range(4):
        start = pl.multiple_of((2 * xx + yl) * CHUNK, CHUNK)
        locals_.append(
            pltpu.make_async_copy(
                ints.at[:, pl.ds(start, CHUNK), :], ints_v.at[xx], lsem.at[1 + xx]
            )
        )
    for copy in locals_:
        copy.start()

    for t in range(3):
        G[z, x, yl, c, t] = coef[:, pl.ds(pl.multiple_of(c * CHUNK + t * 128, 128), 128)]

    barrier = pltpu.get_barrier_semaphore()

    def greet(target):
        pl.semaphore_signal(barrier, inc=1, device_id=target, device_id_type=MESH)

    for dz in range(4):
        for k in range(4):
            if dz or k:
                greet(dev((z + dz) % 4, x, basis_at(k), yl))
    for dz in range(4):
        for dx in (1, 2, 3):
            greet(dev((z + dz) % 4, (x + dx) % 4, b, yl))
    greet(dev(z, x, b, oyl))
    greet(dev(z, x, basis_at(2), oyl))
    pl.semaphore_wait(barrier, 29)

    def send(src, dst, ssem, rsem, target):
        copy = pltpu.make_async_remote_copy(
            src_ref=src,
            dst_ref=dst,
            send_sem=ssem,
            recv_sem=rsem,
            device_id=target,
            device_id_type=MESH,
        )
        copy.start()
        return copy

    sent = []


    def gather(phase, n, ref, target):
        copy = send(ref, ref, gs.at[phase, n], gr.at[phase, n], target)
        sent.append(copy)
        return copy

    order = sorted(range(16), key=lambda n: min(n // 4, 4 - n // 4) + min(n % 4, 4 - n % 4))
    direct = {}
    for n in order[1:]:
        target = dev((z + n // 4) % 4, (x + n % 4) % 4, b, yl)
        direct[n] = gather(0, n, G.at[z, x, yl, c], target)
    aside = {}
    onchip = []
    for n in order:
        if n:
            direct[n].wait_recv()
        zz, xx = (z + 4 - n // 4) % 4, (x + 4 - n % 4) % 4
        turn = (yl + zz + xx) % 2
        ref = G.at[zz, xx, yl, c]
        aside[n] = gather(1, n, ref, dev(z, x, 2 * ((yh + turn) % 2) + c, oyl))
        onchip.append(gather(2, n, ref, dev(z, x, partner, yl)))
    for n in order:
        aside[n].wait_recv()
        zz, xx = (z + 4 - n // 4) % 4, (x + 4 - n % 4) % 4
        onchip.append(gather(3, n, G.at[zz, xx, oyl, c], dev(z, x, partner, yl)))
    for copy in onchip:
        copy.wait_recv()
    zp, zm = (z + 1) % 4, (z + 3) % 4
    xp, xm = (x + 1) % 4, (x + 3) % 4

    lane = lax.broadcasted_iota(jnp.int32, (WIDTH, WIDTH), 1)

    def picked(rb):
        sides = []
        for k in range(NNZ):
            off = offs[k, rb]
            keep = mask[k, rb].astype(jnp.float32)
            odd = lax.rem(off, 2).astype(jnp.float32) * keep
            even = keep - odd
            tile = lax.div(off, 2)
            f = lax.div(tile, 6)
            core = lax.div(lax.rem(tile, 6), 3)
            at = (lax.div(f, 4), lax.rem(f, 4))
            got = jnp.concatenate(
                [G[(*at, o, core, lax.rem(tile, 3))] for o in range(2)], axis=0
            ).astype(jnp.float32)
            turned = pltpu.roll(got, 64, 1)
            if k == 0:
                sides.append(got * even + turned * odd)
            else:
                sides.append(got * odd + turned * even)
        return jnp.where(lane < BLK, sides[0], sides[1]).astype(jnp.bfloat16)

    locals_[0].wait()
    for rb in range(MU_DEV // BLK):
        slab = win_in[:, rb * BLK : (rb + 1) * BLK, :].reshape(AUX * BLK, WIDTH)
        got = dot_nt(slab, picked(rb)).astype(jnp.bfloat16)
        for p in range(AUX):
            win[b, rb * BLK : (rb + 1) * BLK, p * WIDTH : (p + 1) * WIDTH] = got[
                p * BLK : (p + 1) * BLK
            ]
    window = [
        send(win.at[b], win.at[b], ws.at[0], wr.at[0], dev(z, x, partner, yl)),
        send(win.at[b], win.at[b], ws.at[1], wr.at[1], dev(z, x, basis_at(2), oyl)),
    ]
    sent.extend(window)

    for xx in range(4):
        locals_[1 + xx].wait()

    @pl.loop(0, 24)
    def _(i):
        xx = i // 6
        r = i % 6
        slab = ints_v[xx, :, pl.ds(pl.multiple_of(r * BLK, BLK), BLK), :]
        weights = picked((2 * xx + yl) * 6 + r)
        got = dot_nt(slab.reshape(AUX * BLK, WIDTH), weights).astype(jnp.bfloat16)
        at = pl.ds(pl.multiple_of(i * BLK, BLK), BLK)
        for p in range(AUX):
            half[at, p * WIDTH : (p + 1) * WIDTH] = got[p * BLK : (p + 1) * BLK]

    def mix(k):
        bb = basis_at(k)

        @pl.loop(0, AUX, unroll=4)
        def _(p):
            at = pl.ds(pl.multiple_of(p * WIDTH, WIDTH), WIDTH)
            got = jnp.dot(win[bb, :, at], table[...], preferred_element_type=jnp.float32)
            got = got.astype(jnp.bfloat16)
            for r in range(4):
                mixed[r // 2, (r % 2) * 128 : (r % 2) * 128 + 128, at] = got[
                    :, r * WIDTH : (r + 1) * WIDTH
                ]

    def dots(k, h):
        @pl.loop(0, 2)
        def _(i):
            at = pl.ds(pl.multiple_of(i * 2 * CHUNK, 2 * CHUNK), 2 * CHUNK)
            got = dot_nt(half[at, :], mixed[h]).reshape(2, CHUNK, 256)
            two = pl.ds(2 * i, 2)
            partf[k, h, two] = got
            part[k, h, two] = got.astype(jnp.bfloat16)

    def piece(ref, k, h, q, s):
        if h == 0:
            return ref.at[k, h, q, pl.ds(s * 192, 192)]
        return ref.at[k, h, :, pl.ds(pl.multiple_of(q * QUART + s * 48, 16), 48)]

    def recv_one(k, h, side):
        return (r1a if h == 0 else r1b).at[k, side]

    def recv_two(k, h, side, s):
        return (r2a if h == 0 else r2b).at[k, side, s]

    flights = {}

    def ring(axis):
        if axis == 0:
            return x, lambda d: dev(z, (x + d) % 4, b, yl)
        return z, lambda d: dev((z + d) % 4, x, b, yl)

    def launch(k, h):
        me, peer = ring(h)
        got = {}
        for side in range(2):
            got["one", side] = send(
                piece(part, k, h, (me + 2) % 4, side), recv_one(k, h, side),
                s1s.at[k, h, side], s1r.at[k, h, side], peer(1 + 2 * side),
            )
        for side in range(2):
            got["two", side, 1 - side] = send(
                piece(part, k, h, (me + 1 + 2 * side) % 4, 1 - side),
                recv_two(k, h, side, 1 - side),
                s2s.at[k, h, side, 1 - side], s2r.at[k, h, side, 1 - side],
                peer(1 + 2 * side),
            )
        flights[k, h] = got

    def relay(k, h):
        me, peer = ring(h)
        got = flights[k, h]
        for side in range(2):
            got["one", side].wait_recv()
            at = (me + 1 + 2 * side) % 4
            total = piece(partf, k, h, at, side)[...]
            total += recv_one(k, h, side)[...].astype(jnp.float32)
            piece(part, k, h, at, side)[...] = total.astype(jnp.bfloat16)
            got["two", side, side] = send(
                piece(part, k, h, at, side), recv_two(k, h, side, side),
                s2s.at[k, h, side, side], s2r.at[k, h, side, side], peer(1 + 2 * side),
            )

    def own(ref, k, h, q):
        return ref.at[k, h, x, rows(q)] if h == 0 else ref.at[k, h, q, rows(z)]

    def collect(k, h):
        me, _ = ring(h)
        got = flights[k, h]
        for s in range(2):
            got["two", 0, s].wait_recv()
            got["two", 1, s].wait_recv()
            total = piece(partf, k, h, me, s)[...]
            total += recv_two(k, h, 0, s)[...].astype(jnp.float32)
            total += recv_two(k, h, 1, s)[...].astype(jnp.float32)
            piece(partf, k, h, me, s)[...] = total
            piece(part, k, h, me, s)[...] = total.astype(jnp.bfloat16)
        me, peer = ring(1 - h)
        for d in (2, 1, 3):
            got["far", d] = send(
                own(part, k, h, (me + d) % 4), quarter.at[k, h, d - 1],
                qs.at[k, h, d - 1], qr.at[k, h, d - 1], peer(d),
            )

    def finish(k, h):
        me, _ = ring(1 - h)
        got = flights[k, h]
        total = own(partf, k, h, me)[...]
        for d in (1, 3, 2):
            got["far", d].wait_recv()
            total += quarter[k, h, d - 1].astype(jnp.float32)
        fin[k, :, h * 256 : (h + 1) * 256] = total.astype(jnp.bfloat16)

    finals = []

    def deliver(k):
        target = dev(b, x, basis_at(k), yl)
        if k == 0:
            same = z == b

            @pl.when(same)
            def _():
                pltpu.make_async_copy(fin.at[k], last.at[z], tr.at[z]).start()

            @pl.when(jnp.logical_not(same))
            def _():
                send(fin.at[k], last.at[z], ts.at[k], tr.at[z], target)
        else:
            finals.append(send(fin.at[k], last.at[z], ts.at[k], tr.at[z], target))

    order = (0, 2, 3, 1)
    forward = None
    for i, k in enumerate(order):
        if k == 2:
            window[1].wait_recv()
            other = win.at[basis_at(2)]
            forward = send(other, other, ws.at[2], wr.at[2], dev(z, x, partner, yl))
            sent.append(forward)
        elif k == 3:
            forward.wait_recv()
        elif k == 1:
            window[0].wait_recv()
        mix(k)
        for h in (1, 0):
            dots(k, h)
            if i >= 1:
                relay(order[i - 1], h)
            launch(k, h)
            if i >= 2:
                collect(order[i - 2], h)
    for h in range(2):
        relay(order[3], h)
    for h in range(2):
        collect(order[2], h)
    for i in range(2):
        for h in range(2):
            finish(order[i], h)
        deliver(order[i])
    for h in range(2):
        collect(order[3], h)
    for i in range(2, 4):
        for h in range(2):
            finish(order[i], h)
        deliver(order[i])

    for q in range(4):
        pltpu.make_async_copy(fin.at[0], last.at[q], tr.at[q]).wait()
        for r in range(4):
            out[pl.ds(q * CHUNK + r, QUART, stride=4), :] = last[
                q, :, r * MU_DEV : (r + 1) * MU_DEV
            ].astype(jnp.float32)
    for copy in sent:
        copy.wait_send()
    for got in flights.values():
        for copy in got.values():
            copy.wait_send()

    @pl.when(z != b)
    def _():
        pltpu.make_async_remote_copy(
            src_ref=fin.at[0], dst_ref=last.at[z], send_sem=ts.at[0], recv_sem=tr.at[z],
            device_id=dev(b, x, b, yl), device_id_type=MESH,
        ).wait_send()

    for copy in finals:
        copy.wait_send()


def shards(ints, coeffs, offsets, mask):
    table = jnp.asarray(signed_permutations(), jnp.bfloat16)
    bf16, f32 = jnp.bfloat16, jnp.float32
    vmem = pl.BlockSpec(memory_space=pltpu.VMEM)
    smem = pl.BlockSpec(memory_space=pltpu.SMEM)
    dma = pltpu.SemaphoreType.DMA
    result = pl.pallas_call(
        kernel,
        out_shape=jax.ShapeDtypeStruct((4 * CHUNK, MU_DEV), f32),
        in_specs=[pl.BlockSpec(memory_space=pl.ANY), vmem, vmem, smem, smem],
        out_specs=vmem,
        scratch_shapes=[
            pltpu.VMEM((AUX, MU_DEV, WIDTH), bf16),
            pltpu.VMEM((4, AUX, CHUNK, WIDTH), bf16),
            pltpu.VMEM((4, 4, 2, 2, 3, 64, 128), bf16),
            pltpu.VMEM((4, MU_DEV, KDIM), bf16),
            pltpu.VMEM((2, 256, KDIM), bf16),
            pltpu.VMEM((4 * CHUNK, KDIM), bf16),
            pltpu.VMEM((4, 2, 4, CHUNK, 256), bf16),
            pltpu.VMEM((4, 2, 4, CHUNK, 256), f32),
            pltpu.VMEM((4, 2, 192, 256), bf16),
            pltpu.VMEM((4, 2, 4, 48, 256), bf16),
            pltpu.VMEM((4, 2, 2, 192, 256), bf16),
            pltpu.VMEM((4, 2, 2, 4, 48, 256), bf16),
            pltpu.VMEM((4, 2, 3, QUART, 256), bf16),
            pltpu.VMEM((4, QUART, 512), bf16),
            pltpu.VMEM((4, QUART, 512), bf16),
            dma((5,)),
            dma((4, 16)),
            dma((4, 16)),
            dma((3,)),
            dma((3,)),
            dma((4, 2, 2)),
            dma((4, 2, 2)),
            dma((4, 2, 2, 2)),
            dma((4, 2, 2, 2)),
            dma((4, 2, 3)),
            dma((4, 2, 3)),
            dma((4,)),
            dma((4,)),
        ],
        compiler_params=pltpu.CompilerParams(
            collective_id=0, has_side_effects=True, vmem_limit_bytes=60 * 1024 * 1024
        ),
        name="exchange",
    )(ints, coeffs.T, table, offsets.T, mask.T)
    return result.reshape(CHUNK, 4, MU_DEV)


def solution(mesh):
    return jax.shard_map(
        shards,
        mesh=mesh,
        in_specs=(P("fit", "basis", None), P("fit", "occ"), P("basis", None), P("basis", None)),
        out_specs=P(("fit", "occ"), None, "basis"),
        check_vma=False,
    )
```

```python
import functools

import jax
import jax.numpy as jnp
import numpy as np
from jax import lax
from jax.experimental import pallas as pl
from jax.experimental.pallas import tpu as pltpu
from jax.sharding import PartitionSpec as P

BLK = 64
NNZ = 2
MU_DEV = 128
AUX = 16
ROWS = 3072
CHUNK = 384
QUART = 96
WIDTH = 128
KDIM = AUX * WIDTH
MESH = pl.DeviceIdType.MESH
SIGN_ENTRIES = (
    (0, 0, 0, 1),
    (0, 1, 1, 1),
    (0, 2, 2, 1),
    (0, 3, 3, 1),
    (1, 0, 1, -1),
    (1, 1, 0, 1),
    (1, 2, 3, -1),
    (1, 3, 2, 1),
    (2, 0, 2, -1),
    (2, 1, 3, 1),
    (2, 2, 0, 1),
    (2, 3, 1, -1),
    (3, 0, 3, -1),
    (3, 1, 2, -1),
    (3, 2, 1, 1),
    (3, 3, 0, 1),
)


def signed_permutations():
    table = np.zeros((WIDTH, 4, WIDTH), np.float32)
    for r, q, s, sign in SIGN_ENTRIES:
        for i in range(WIDTH // 4):
            table[4 * i + q, r, 4 * i + s] = sign
    return table.reshape(WIDTH, 4 * WIDTH)


def dot_nt(a, b):
    return lax.dot_general(
        a, b, (((1,), (1,)), ((), ())), preferred_element_type=jnp.float32
    )


def kernel(
    ints, coef, table, offs, mask, out,
    win_in, ints_v, G, win, mixed, half, part, partf,
    r1a, r1b, r2a, r2b, quarter, fin, last,
    lsem, gs, gr, ws, wr, s1s, s1r, s2s, s2r, qs, qr, ts, tr,
):
    fit = lax.axis_index("fit")
    b = lax.axis_index("basis")
    yl = lax.axis_index("occ")
    z = fit // 4
    x = fit % 4
    yh = b // 2
    c = b % 2
    oyl = 1 - yl
    partner = 2 * yh + (1 - c)

    def basis_at(k):
        return 2 * ((yh + k // 2) % 2) + (c + k % 2) % 2

    def dev(zz, xx, bb, ll):
        return (zz * 4 + xx, bb, ll)

    def rows(q):
        return pl.ds(pl.multiple_of(q * QUART, QUART), QUART)

    locals_ = [pltpu.make_async_copy(ints.at[:, pl.ds(0, MU_DEV), :], win_in, lsem.at[0])]
    for xx in range(4):
        start = pl.multiple_of((2 * xx + yl) * CHUNK, CHUNK)
        locals_.append(
            pltpu.make_async_copy(
                ints.at[:, pl.ds(start, CHUNK), :], ints_v.at[xx], lsem.at[1 + xx]
            )
        )
    for copy in locals_:
        copy.start()

    for t in range(3):
        G[z, x, yl, c, t] = coef[:, pl.ds(pl.multiple_of(c * CHUNK + t * 128, 128), 128)]

    barrier = pltpu.get_barrier_semaphore()

    def greet(target):
        pl.semaphore_signal(barrier, inc=1, device_id=target, device_id_type=MESH)

    for d in (1, 2, 3):
        greet(dev(z, (x + d) % 4, b, yl))
        greet(dev((z + d) % 4, x, b, yl))
    greet(dev(z, x, b, oyl))
    greet(dev(z, x, basis_at(2), oyl))
    greet(dev(z, x, partner, yl))
    pl.semaphore_wait(barrier, 9)

    def send(src, dst, ssem, rsem, target):
        copy = pltpu.make_async_remote_copy(
            src_ref=src,
            dst_ref=dst,
            send_sem=ssem,
            recv_sem=rsem,
            device_id=target,
            device_id_type=MESH,
        )
        copy.start()
        return copy

    sent = []


    near = (1, 3, 2)
    colors = (0, 1)

    def half_piece(color, first, second, o):
        dx, dz = (first, second) if color == 0 else (second, first)
        at = (z + 4 - dz) % 4, (x + 4 - dx) % 4
        return G.at[(*at, o, c)].at[:, pl.ds(32 * color, 32), :]

    def half_group(color, second, o):
        if color == 0:
            return G.at[(z + 4 - second) % 4, :, o, c, :, pl.ds(0, 32), :]
        return G.at[:, (x + 4 - second) % 4, o, c, :, pl.ds(32, 32), :]

    def along(axis, d):
        return dev(z, (x + d) % 4, b, yl) if axis == 0 else dev((z + d) % 4, x, b, yl)

    def gather(phase, color, m, d, ref, target):
        n = m * 4 + d
        copy = send(ref, ref, gs.at[phase, color, n], gr.at[phase, color, n], target)
        sent.append(copy)
        return copy

    one, two, side_y, onchip = {}, {}, {}, []

    def second_stage(color, m):
        for d in near:
            two[color, m, d] = gather(
                1, color, m, d, half_piece(color, m, 0, yl), along(1 - color, d)
            )

    def pair(color, d, o, phase):
        onchip.append(
            gather(phase, color, 0, d, half_group(color, d, o), dev(z, x, partner, yl))
        )

    def outward(color, m, d):
        turn = (yl + color) % 2
        side_y[color, m, d] = gather(
            2, color, m, d, half_piece(color, m, d, yl),
            dev(z, x, 2 * ((yh + turn) % 2) + c, oyl),
        )

    for d in near:
        for color in colors:
            one[color, d] = gather(
                0, color, 0, d, half_piece(color, 0, 0, yl), along(color, d)
            )
    for color in colors:
        second_stage(color, 0)
        outward(color, 0, 0)
    for m in near:
        for color in colors:
            one[color, m].wait_recv()
            second_stage(color, m)
            outward(color, m, 0)
    for m in (0, 1, 3, 2):
        for d in near:
            for color in colors:
                two[color, m, d].wait_recv()
                outward(color, m, d)
    for d in (0, 1, 3, 2):
        for color in colors:
            pair(color, d, yl, 3)
    for d in (0, 1, 3, 2):
        for color in colors:
            for m in (0, 1, 3, 2):
                side_y[color, m, d].wait_recv()
            pair(color, d, oyl, 4)
    for copy in onchip:
        copy.wait_recv()
    zp, zm = (z + 1) % 4, (z + 3) % 4
    xp, xm = (x + 1) % 4, (x + 3) % 4

    lane = lax.broadcasted_iota(jnp.int32, (WIDTH, WIDTH), 1)

    def picked(rb):
        sides = []
        for k in range(NNZ):
            off = offs[k, rb]
            keep = mask[k, rb].astype(jnp.float32)
            odd = lax.rem(off, 2).astype(jnp.float32) * keep
            even = keep - odd
            tile = lax.div(off, 2)
            f = lax.div(tile, 6)
            core = lax.div(lax.rem(tile, 6), 3)
            at = (lax.div(f, 4), lax.rem(f, 4))
            got = jnp.concatenate(
                [G[(*at, o, core, lax.rem(tile, 3))] for o in range(2)], axis=0
            ).astype(jnp.float32)
            turned = pltpu.roll(got, 64, 1)
            if k == 0:
                sides.append(got * even + turned * odd)
            else:
                sides.append(got * odd + turned * even)
        return jnp.where(lane < BLK, sides[0], sides[1]).astype(jnp.bfloat16)

    locals_[0].wait()
    for rb in range(MU_DEV // BLK):
        slab = win_in[:, rb * BLK : (rb + 1) * BLK, :].reshape(AUX * BLK, WIDTH)
        got = dot_nt(slab, picked(rb)).astype(jnp.bfloat16)
        for p in range(AUX):
            win[b, rb * BLK : (rb + 1) * BLK, p * WIDTH : (p + 1) * WIDTH] = got[
                p * BLK : (p + 1) * BLK
            ]
    window = [
        send(win.at[b], win.at[b], ws.at[0], wr.at[0], dev(z, x, partner, yl)),
        send(win.at[b], win.at[b], ws.at[1], wr.at[1], dev(z, x, basis_at(2), oyl)),
    ]
    sent.extend(window)

    for xx in range(4):
        locals_[1 + xx].wait()

    @pl.loop(0, 24, unroll=8)
    def _(i):
        xx = i // 6
        r = i % 6
        slab = ints_v[xx, :, pl.ds(pl.multiple_of(r * BLK, BLK), BLK), :]
        weights = picked((2 * xx + yl) * 6 + r)
        got = dot_nt(slab.reshape(AUX * BLK, WIDTH), weights).astype(jnp.bfloat16)
        at = pl.ds(pl.multiple_of(i * BLK, BLK), BLK)
        for p in range(AUX):
            half[at, p * WIDTH : (p + 1) * WIDTH] = got[p * BLK : (p + 1) * BLK]

    def mix(k):
        bb = basis_at(k)

        @pl.loop(0, AUX, unroll=4)
        def _(p):
            at = pl.ds(pl.multiple_of(p * WIDTH, WIDTH), WIDTH)
            got = jnp.dot(win[bb, :, at], table[...], preferred_element_type=jnp.float32)
            got = got.astype(jnp.bfloat16)
            for r in range(4):
                mixed[r // 2, (r % 2) * 128 : (r % 2) * 128 + 128, at] = got[
                    :, r * WIDTH : (r + 1) * WIDTH
                ]

    def dots(k, h):
        @pl.loop(0, 2)
        def _(i):
            at = pl.ds(pl.multiple_of(i * 2 * CHUNK, 2 * CHUNK), 2 * CHUNK)
            got = dot_nt(half[at, :], mixed[h]).reshape(2, CHUNK, 256)
            two = pl.ds(2 * i, 2)
            partf[k, h, two] = got
            part[k, h, two] = got.astype(jnp.bfloat16)

    def piece(ref, k, h, q, s):
        if h == 0:
            return ref.at[k, h, q, pl.ds(s * 192, 192)]
        return ref.at[k, h, :, pl.ds(pl.multiple_of(q * QUART + s * 48, 16), 48)]

    def recv_one(k, h, side):
        return (r1a if h == 0 else r1b).at[k, side]

    def recv_two(k, h, side, s):
        return (r2a if h == 0 else r2b).at[k, side, s]

    flights = {}

    def ring(axis):
        if axis == 0:
            return x, lambda d: dev(z, (x + d) % 4, b, yl)
        return z, lambda d: dev((z + d) % 4, x, b, yl)

    def launch(k, h):
        me, peer = ring(h)
        got = {}
        for side in range(2):
            got["one", side] = send(
                piece(part, k, h, (me + 2) % 4, side), recv_one(k, h, side),
                s1s.at[k, h, side], s1r.at[k, h, side], peer(1 + 2 * side),
            )
        for side in range(2):
            got["two", side, 1 - side] = send(
                piece(part, k, h, (me + 1 + 2 * side) % 4, 1 - side),
                recv_two(k, h, side, 1 - side),
                s2s.at[k, h, side, 1 - side], s2r.at[k, h, side, 1 - side],
                peer(1 + 2 * side),
            )
        flights[k, h] = got

    def relay(k, h):
        me, peer = ring(h)
        got = flights[k, h]
        for side in range(2):
            got["one", side].wait_recv()
            at = (me + 1 + 2 * side) % 4
            total = piece(partf, k, h, at, side)[...]
            total += recv_one(k, h, side)[...].astype(jnp.float32)
            piece(part, k, h, at, side)[...] = total.astype(jnp.bfloat16)
            got["two", side, side] = send(
                piece(part, k, h, at, side), recv_two(k, h, side, side),
                s2s.at[k, h, side, side], s2r.at[k, h, side, side], peer(1 + 2 * side),
            )

    def own(ref, k, h, q):
        return ref.at[k, h, x, rows(q)] if h == 0 else ref.at[k, h, q, rows(z)]

    def collect(k, h):
        me, _ = ring(h)
        got = flights[k, h]
        for s in range(2):
            got["two", 0, s].wait_recv()
            got["two", 1, s].wait_recv()
            total = piece(partf, k, h, me, s)[...]
            total += recv_two(k, h, 0, s)[...].astype(jnp.float32)
            total += recv_two(k, h, 1, s)[...].astype(jnp.float32)
            piece(partf, k, h, me, s)[...] = total
            piece(part, k, h, me, s)[...] = total.astype(jnp.bfloat16)
        me, peer = ring(1 - h)
        for d in (2, 1, 3):
            got["far", d] = send(
                own(part, k, h, (me + d) % 4), quarter.at[k, h, d - 1],
                qs.at[k, h, d - 1], qr.at[k, h, d - 1], peer(d),
            )

    def finish(k, h):
        me, _ = ring(1 - h)
        got = flights[k, h]
        total = own(partf, k, h, me)[...]
        for d in (1, 3, 2):
            got["far", d].wait_recv()
            total += quarter[k, h, d - 1].astype(jnp.float32)
        fin[k, :, h * 256 : (h + 1) * 256] = total.astype(jnp.bfloat16)

    finals = []

    def deliver(k):
        target = dev(b, x, basis_at(k), yl)
        if k == 0:
            same = z == b

            @pl.when(same)
            def _():
                pltpu.make_async_copy(fin.at[k], last.at[z], tr.at[z]).start()

            @pl.when(jnp.logical_not(same))
            def _():
                send(fin.at[k], last.at[z], ts.at[k], tr.at[z], target)
        else:
            finals.append(send(fin.at[k], last.at[z], ts.at[k], tr.at[z], target))

    order = (0, 1, 2, 3)
    forward = None
    for i, k in enumerate(order):
        if k == 2:
            window[1].wait_recv()
            other = win.at[basis_at(2)]
            forward = send(other, other, ws.at[2], wr.at[2], dev(z, x, partner, yl))
            sent.append(forward)
        elif k == 3:
            forward.wait_recv()
        elif k == 1:
            window[0].wait_recv()
        mix(k)
        for h in (1, 0):
            dots(k, h)
            if i >= 1:
                relay(order[i - 1], h)
            launch(k, h)
            if i >= 2:
                collect(order[i - 2], h)
    for h in range(2):
        relay(order[3], h)
    for h in range(2):
        collect(order[2], h)
    for i in range(2):
        for h in range(2):
            finish(order[i], h)
        deliver(order[i])
    for h in range(2):
        collect(order[3], h)
    for i in range(2, 4):
        for h in range(2):
            finish(order[i], h)
        deliver(order[i])

    for q in range(4):
        pltpu.make_async_copy(fin.at[0], last.at[q], tr.at[q]).wait()
        for r in range(4):
            out[pl.ds(q * CHUNK + r, QUART, stride=4), :] = last[
                q, :, r * MU_DEV : (r + 1) * MU_DEV
            ].astype(jnp.float32)
    for copy in sent:
        copy.wait_send()
    for got in flights.values():
        for copy in got.values():
            copy.wait_send()

    @pl.when(z != b)
    def _():
        pltpu.make_async_remote_copy(
            src_ref=fin.at[0], dst_ref=last.at[z], send_sem=ts.at[0], recv_sem=tr.at[z],
            device_id=dev(b, x, b, yl), device_id_type=MESH,
        ).wait_send()

    for copy in finals:
        copy.wait_send()


def shards(ints, coeffs, offsets, mask):
    table = jnp.asarray(signed_permutations(), jnp.bfloat16)
    bf16, f32 = jnp.bfloat16, jnp.float32
    vmem = pl.BlockSpec(memory_space=pltpu.VMEM)
    smem = pl.BlockSpec(memory_space=pltpu.SMEM)
    dma = pltpu.SemaphoreType.DMA
    result = pl.pallas_call(
        kernel,
        out_shape=jax.ShapeDtypeStruct((4 * CHUNK, MU_DEV), f32),
        in_specs=[pl.BlockSpec(memory_space=pl.ANY), vmem, vmem, smem, smem],
        out_specs=vmem,
        scratch_shapes=[
            pltpu.VMEM((AUX, MU_DEV, WIDTH), bf16),
            pltpu.VMEM((4, AUX, CHUNK, WIDTH), bf16),
            pltpu.VMEM((4, 4, 2, 2, 3, 64, 128), bf16),
            pltpu.VMEM((4, MU_DEV, KDIM), bf16),
            pltpu.VMEM((2, 256, KDIM), bf16),
            pltpu.VMEM((4 * CHUNK, KDIM), bf16),
            pltpu.VMEM((4, 2, 4, CHUNK, 256), bf16),
            pltpu.VMEM((4, 2, 4, CHUNK, 256), f32),
            pltpu.VMEM((4, 2, 192, 256), bf16),
            pltpu.VMEM((4, 2, 4, 48, 256), bf16),
            pltpu.VMEM((4, 2, 2, 192, 256), bf16),
            pltpu.VMEM((4, 2, 2, 4, 48, 256), bf16),
            pltpu.VMEM((4, 2, 3, QUART, 256), bf16),
            pltpu.VMEM((4, QUART, 512), bf16),
            pltpu.VMEM((4, QUART, 512), bf16),
            dma((5,)),
            dma((5, 2, 16)),
            dma((5, 2, 16)),
            dma((3,)),
            dma((3,)),
            dma((4, 2, 2)),
            dma((4, 2, 2)),
            dma((4, 2, 2, 2)),
            dma((4, 2, 2, 2)),
            dma((4, 2, 3)),
            dma((4, 2, 3)),
            dma((4,)),
            dma((4,)),
        ],
        compiler_params=pltpu.CompilerParams(
            collective_id=0, has_side_effects=True, vmem_limit_bytes=60 * 1024 * 1024
        ),
        name="exchange",
    )(ints, coeffs.T, table, offsets.T, mask.T)
    return result.reshape(CHUNK, 4, MU_DEV)


def solution(mesh):
    return jax.shard_map(
        shards,
        mesh=mesh,
        in_specs=(P("fit", "basis", None), P("fit", "occ"), P("basis", None), P("basis", None)),
        out_specs=P(("fit", "occ"), None, "basis"),
        check_vma=False,
    )
```

```python
import functools

import jax
import jax.numpy as jnp
import numpy as np
from jax import lax
from jax.experimental import pallas as pl
from jax.experimental.pallas import tpu as pltpu
from jax.sharding import PartitionSpec as P

BLK = 64
NNZ = 2
MU_DEV = 128
AUX = 16
ROWS = 3072
CHUNK = 384
QUART = 96
WIDTH = 128
KDIM = AUX * WIDTH
MESH = pl.DeviceIdType.MESH
UNITS = tuple((k, h) for k in range(4) for h in range(2))
X_FIRST = ((0, 0), (1, 0), (2, 0), (3, 0))
N_X = len(X_FIRST)
N_Z = len(UNITS) - N_X
H_ORDER = (0, 1)
SIGN_ENTRIES = (
    (0, 0, 0, 1),
    (0, 1, 1, 1),
    (0, 2, 2, 1),
    (0, 3, 3, 1),
    (1, 0, 1, -1),
    (1, 1, 0, 1),
    (1, 2, 3, -1),
    (1, 3, 2, 1),
    (2, 0, 2, -1),
    (2, 1, 3, 1),
    (2, 2, 0, 1),
    (2, 3, 1, -1),
    (3, 0, 3, -1),
    (3, 1, 2, -1),
    (3, 2, 1, 1),
    (3, 3, 0, 1),
)


def signed_permutations():
    table = np.zeros((WIDTH, 4, WIDTH), np.float32)
    for r, q, s, sign in SIGN_ENTRIES:
        for i in range(WIDTH // 4):
            table[4 * i + q, r, 4 * i + s] = sign
    return table.reshape(WIDTH, 4 * WIDTH)


def dot_nt(a, b):
    return lax.dot_general(
        a, b, (((1,), (1,)), ((), ())), preferred_element_type=jnp.float32
    )


def kernel(
    ints, coef, table, offs, mask, out,
    win_in, ints_v, G, win, mixed, half, part, partf,
    r1a, r1b, r2a, r2b, quarter, fin, last,
    lsem, gs, gr, ws, wr, s1s, s1r, s2s, s2r, qs, qr, ts, tr,
):
    fit = lax.axis_index("fit")
    b = lax.axis_index("basis")
    yl = lax.axis_index("occ")
    z = fit // 4
    x = fit % 4
    yh = b // 2
    c = b % 2
    oyl = 1 - yl
    partner = 2 * yh + (1 - c)

    def basis_at(k):
        return 2 * ((yh + k // 2) % 2) + (c + k % 2) % 2

    def dev(zz, xx, bb, ll):
        return (zz * 4 + xx, bb, ll)

    def rows(q):
        return pl.ds(pl.multiple_of(q * QUART, QUART), QUART)

    locals_ = [pltpu.make_async_copy(ints.at[:, pl.ds(0, MU_DEV), :], win_in, lsem.at[0])]
    for xx in range(4):
        start = pl.multiple_of((2 * xx + yl) * CHUNK, CHUNK)
        locals_.append(
            pltpu.make_async_copy(
                ints.at[:, pl.ds(start, CHUNK), :], ints_v.at[xx], lsem.at[1 + xx]
            )
        )
    for copy in locals_:
        copy.start()

    for t in range(3):
        G[z, x, yl, c, t] = coef[:, pl.ds(pl.multiple_of(c * CHUNK + t * 128, 128), 128)]

    barrier = pltpu.get_barrier_semaphore()

    def greet(target):
        pl.semaphore_signal(barrier, inc=1, device_id=target, device_id_type=MESH)

    for d in (1, 2, 3):
        greet(dev(z, (x + d) % 4, b, yl))
        greet(dev((z + d) % 4, x, b, yl))
    greet(dev(z, x, b, oyl))
    greet(dev(z, x, basis_at(2), oyl))
    greet(dev(z, x, partner, yl))
    pl.semaphore_wait(barrier, 9)

    def send(src, dst, ssem, rsem, target):
        copy = pltpu.make_async_remote_copy(
            src_ref=src,
            dst_ref=dst,
            send_sem=ssem,
            recv_sem=rsem,
            device_id=target,
            device_id_type=MESH,
        )
        copy.start()
        return copy

    sent = []


    near = (1, 3, 2)
    colors = (0, 1)

    def half_piece(color, first, second, o):
        dx, dz = (first, second) if color == 0 else (second, first)
        at = (z + 4 - dz) % 4, (x + 4 - dx) % 4
        return G.at[(*at, o, c)].at[:, pl.ds(32 * color, 32), :]

    def half_group(color, second, o):
        if color == 0:
            return G.at[(z + 4 - second) % 4, :, o, c, :, pl.ds(0, 32), :]
        return G.at[:, (x + 4 - second) % 4, o, c, :, pl.ds(32, 32), :]

    def along(axis, d):
        return dev(z, (x + d) % 4, b, yl) if axis == 0 else dev((z + d) % 4, x, b, yl)

    def gather(phase, color, m, d, ref, target):
        n = m * 4 + d
        copy = send(ref, ref, gs.at[phase, color, n], gr.at[phase, color, n], target)
        sent.append(copy)
        return copy

    one, two, side_y, onchip = {}, {}, {}, []

    def second_stage(color, m):
        for d in near:
            two[color, m, d] = gather(
                1, color, m, d, half_piece(color, m, 0, yl), along(1 - color, d)
            )

    def pair(color, d, o, phase):
        onchip.append(
            gather(phase, color, 0, d, half_group(color, d, o), dev(z, x, partner, yl))
        )

    def outward(color, m, d):
        turn = (yl + color) % 2
        side_y[color, m, d] = gather(
            2, color, m, d, half_piece(color, m, d, yl),
            dev(z, x, 2 * ((yh + turn) % 2) + c, oyl),
        )

    for d in near:
        for color in colors:
            one[color, d] = gather(
                0, color, 0, d, half_piece(color, 0, 0, yl), along(color, d)
            )
    for color in colors:
        second_stage(color, 0)
        outward(color, 0, 0)
    for m in near:
        for color in colors:
            one[color, m].wait_recv()
            second_stage(color, m)
            outward(color, m, 0)
    for m in (0, 1, 3, 2):
        for d in near:
            for color in colors:
                two[color, m, d].wait_recv()
                outward(color, m, d)
    for d in (0, 1, 3, 2):
        for color in colors:
            pair(color, d, yl, 3)
    for d in (0, 1, 3, 2):
        for color in colors:
            for m in (0, 1, 3, 2):
                side_y[color, m, d].wait_recv()
            pair(color, d, oyl, 4)
    for copy in onchip:
        copy.wait_recv()
    zp, zm = (z + 1) % 4, (z + 3) % 4
    xp, xm = (x + 1) % 4, (x + 3) % 4

    lane = lax.broadcasted_iota(jnp.int32, (WIDTH, WIDTH), 1)

    def picked(rb):
        sides = []
        for k in range(NNZ):
            off = offs[k, rb]
            keep = mask[k, rb].astype(jnp.float32)
            odd = lax.rem(off, 2).astype(jnp.float32) * keep
            even = keep - odd
            tile = lax.div(off, 2)
            f = lax.div(tile, 6)
            core = lax.div(lax.rem(tile, 6), 3)
            at = (lax.div(f, 4), lax.rem(f, 4))
            got = jnp.concatenate(
                [G[(*at, o, core, lax.rem(tile, 3))] for o in range(2)], axis=0
            ).astype(jnp.float32)
            turned = pltpu.roll(got, 64, 1)
            if k == 0:
                sides.append(got * even + turned * odd)
            else:
                sides.append(got * odd + turned * even)
        return jnp.where(lane < BLK, sides[0], sides[1]).astype(jnp.bfloat16)

    locals_[0].wait()
    for rb in range(MU_DEV // BLK):
        slab = win_in[:, rb * BLK : (rb + 1) * BLK, :].reshape(AUX * BLK, WIDTH)
        got = dot_nt(slab, picked(rb)).astype(jnp.bfloat16)
        for p in range(AUX):
            win[b, rb * BLK : (rb + 1) * BLK, p * WIDTH : (p + 1) * WIDTH] = got[
                p * BLK : (p + 1) * BLK
            ]
    window = [
        send(win.at[b], win.at[b], ws.at[0], wr.at[0], dev(z, x, partner, yl)),
        send(win.at[b], win.at[b], ws.at[1], wr.at[1], dev(z, x, basis_at(2), oyl)),
    ]
    sent.extend(window)

    for xx in range(4):
        locals_[1 + xx].wait()

    @pl.loop(0, 24, unroll=8)
    def _(i):
        xx = i // 6
        r = i % 6
        slab = ints_v[xx, :, pl.ds(pl.multiple_of(r * BLK, BLK), BLK), :]
        weights = picked((2 * xx + yl) * 6 + r)
        got = dot_nt(slab.reshape(AUX * BLK, WIDTH), weights).astype(jnp.bfloat16)
        at = pl.ds(pl.multiple_of(i * BLK, BLK), BLK)
        for p in range(AUX):
            half[at, p * WIDTH : (p + 1) * WIDTH] = got[p * BLK : (p + 1) * BLK]

    def mix(k):
        bb = basis_at(k)

        @pl.loop(0, AUX, unroll=16)
        def _(p):
            at = pl.ds(pl.multiple_of(p * WIDTH, WIDTH), WIDTH)
            got = jnp.dot(win[bb, :, at], table[...], preferred_element_type=jnp.float32)
            got = got.astype(jnp.bfloat16)
            for r in range(4):
                mixed[r // 2, (r % 2) * 128 : (r % 2) * 128 + 128, at] = got[
                    :, r * WIDTH : (r + 1) * WIDTH
                ]

    def dots(k, h):
        @pl.loop(0, 2)
        def _(i):
            at = pl.ds(pl.multiple_of(i * 2 * CHUNK, 2 * CHUNK), 2 * CHUNK)
            got = dot_nt(half[at, :], mixed[h]).reshape(2, CHUNK, 256)
            two = pl.ds(2 * i, 2)
            partf[k, h, two] = got
            part[k, h, two] = got.astype(jnp.bfloat16)

    def color_of(k, h):
        return 0 if (k, h) in X_FIRST else 1

    def slot(k, h):
        same = [u for u in UNITS if color_of(*u) == color_of(k, h)]
        return same.index((k, h))

    def piece(ref, k, h, q, s):
        if color_of(k, h) == 0:
            return ref.at[k, h, q, pl.ds(s * 192, 192)]
        return ref.at[k, h, :, pl.ds(pl.multiple_of(q * QUART + s * 48, 16), 48)]

    def recv_one(k, h, side):
        return (r1a, r1b)[color_of(k, h)].at[slot(k, h), side]

    def recv_two(k, h, side, s):
        return (r2a, r2b)[color_of(k, h)].at[slot(k, h), side, s]

    flights = {}

    def ring(axis):
        if axis == 0:
            return x, lambda d: dev(z, (x + d) % 4, b, yl)
        return z, lambda d: dev((z + d) % 4, x, b, yl)

    def launch(k, h):
        me, peer = ring(color_of(k, h))
        got = {}
        for side in range(2):
            got["one", side] = send(
                piece(part, k, h, (me + 2) % 4, side), recv_one(k, h, side),
                s1s.at[k, h, side], s1r.at[k, h, side], peer(1 + 2 * side),
            )
        for side in range(2):
            got["two", side, 1 - side] = send(
                piece(part, k, h, (me + 1 + 2 * side) % 4, 1 - side),
                recv_two(k, h, side, 1 - side),
                s2s.at[k, h, side, 1 - side], s2r.at[k, h, side, 1 - side],
                peer(1 + 2 * side),
            )
        flights[k, h] = got

    def relay(k, h):
        me, peer = ring(color_of(k, h))
        got = flights[k, h]
        for side in range(2):
            got["one", side].wait_recv()
            at = (me + 1 + 2 * side) % 4
            total = piece(partf, k, h, at, side)[...]
            total += recv_one(k, h, side)[...].astype(jnp.float32)
            piece(part, k, h, at, side)[...] = total.astype(jnp.bfloat16)
            got["two", side, side] = send(
                piece(part, k, h, at, side), recv_two(k, h, side, side),
                s2s.at[k, h, side, side], s2r.at[k, h, side, side], peer(1 + 2 * side),
            )

    def own(ref, k, h, q):
        if color_of(k, h) == 0:
            return ref.at[k, h, x, rows(q)]
        return ref.at[k, h, q, rows(z)]

    def collect(k, h):
        me, _ = ring(color_of(k, h))
        got = flights[k, h]
        for s in range(2):
            got["two", 0, s].wait_recv()
            got["two", 1, s].wait_recv()
            total = piece(partf, k, h, me, s)[...]
            total += recv_two(k, h, 0, s)[...].astype(jnp.float32)
            total += recv_two(k, h, 1, s)[...].astype(jnp.float32)
            piece(partf, k, h, me, s)[...] = total
            piece(part, k, h, me, s)[...] = total.astype(jnp.bfloat16)
        me, peer = ring(1 - color_of(k, h))
        for d in (2, 1, 3):
            got["far", d] = send(
                own(part, k, h, (me + d) % 4), quarter.at[k, h, d - 1],
                qs.at[k, h, d - 1], qr.at[k, h, d - 1], peer(d),
            )

    def finish(k, h):
        me, _ = ring(1 - color_of(k, h))
        got = flights[k, h]
        total = own(partf, k, h, me)[...]
        for d in (1, 3, 2):
            got["far", d].wait_recv()
            total += quarter[k, h, d - 1].astype(jnp.float32)
        fin[k, :, h * 256 : (h + 1) * 256] = total.astype(jnp.bfloat16)

    finals = []

    def deliver(k):
        target = dev(b, x, basis_at(k), yl)
        if k == 0:
            same = z == b

            @pl.when(same)
            def _():
                pltpu.make_async_copy(fin.at[k], last.at[z], tr.at[z]).start()

            @pl.when(jnp.logical_not(same))
            def _():
                send(fin.at[k], last.at[z], ts.at[k], tr.at[z], target)
        else:
            finals.append(send(fin.at[k], last.at[z], ts.at[k], tr.at[z], target))

    order = (0, 1, 2, 3)
    forward = None
    for i, k in enumerate(order):
        if k == 2:
            window[1].wait_recv()
            other = win.at[basis_at(2)]
            forward = send(other, other, ws.at[2], wr.at[2], dev(z, x, partner, yl))
            sent.append(forward)
        elif k == 3:
            forward.wait_recv()
        elif k == 1:
            window[0].wait_recv()
        mix(k)
        for h in H_ORDER:
            dots(k, h)
            if i >= 1:
                relay(order[i - 1], h)
            launch(k, h)
            if i >= 2:
                collect(order[i - 2], h)
    for h in range(2):
        relay(order[3], h)
    for h in range(2):
        collect(order[2], h)
    for h in range(2):
        collect(order[3], h)
    for i in range(4):
        for h in range(2):
            finish(order[i], h)
        deliver(order[i])

    for q in range(4):
        pltpu.make_async_copy(fin.at[0], last.at[q], tr.at[q]).wait()
        for r in range(4):
            out[pl.ds(q * CHUNK + r, QUART, stride=4), :] = last[
                q, :, r * MU_DEV : (r + 1) * MU_DEV
            ].astype(jnp.float32)
    for copy in sent:
        copy.wait_send()
    for got in flights.values():
        for copy in got.values():
            copy.wait_send()

    @pl.when(z != b)
    def _():
        pltpu.make_async_remote_copy(
            src_ref=fin.at[0], dst_ref=last.at[z], send_sem=ts.at[0], recv_sem=tr.at[z],
            device_id=dev(b, x, b, yl), device_id_type=MESH,
        ).wait_send()

    for copy in finals:
        copy.wait_send()


def shards(ints, coeffs, offsets, mask):
    table = jnp.asarray(signed_permutations(), jnp.bfloat16)
    bf16, f32 = jnp.bfloat16, jnp.float32
    vmem = pl.BlockSpec(memory_space=pltpu.VMEM)
    smem = pl.BlockSpec(memory_space=pltpu.SMEM)
    dma = pltpu.SemaphoreType.DMA
    result = pl.pallas_call(
        kernel,
        out_shape=jax.ShapeDtypeStruct((4 * CHUNK, MU_DEV), f32),
        in_specs=[pl.BlockSpec(memory_space=pl.ANY), vmem, vmem, smem, smem],
        out_specs=vmem,
        scratch_shapes=[
            pltpu.VMEM((AUX, MU_DEV, WIDTH), bf16),
            pltpu.VMEM((4, AUX, CHUNK, WIDTH), bf16),
            pltpu.VMEM((4, 4, 2, 2, 3, 64, 128), bf16),
            pltpu.VMEM((4, MU_DEV, KDIM), bf16),
            pltpu.VMEM((2, 256, KDIM), bf16),
            pltpu.VMEM((4 * CHUNK, KDIM), bf16),
            pltpu.VMEM((4, 2, 4, CHUNK, 256), bf16),
            pltpu.VMEM((4, 2, 4, CHUNK, 256), f32),
            pltpu.VMEM((N_X, 2, 192, 256), bf16),
            pltpu.VMEM((N_Z, 2, 4, 48, 256), bf16),
            pltpu.VMEM((N_X, 2, 2, 192, 256), bf16),
            pltpu.VMEM((N_Z, 2, 2, 4, 48, 256), bf16),
            pltpu.VMEM((4, 2, 3, QUART, 256), bf16),
            pltpu.VMEM((4, QUART, 512), bf16),
            pltpu.VMEM((4, QUART, 512), bf16),
            dma((5,)),
            dma((5, 2, 16)),
            dma((5, 2, 16)),
            dma((3,)),
            dma((3,)),
            dma((4, 2, 2)),
            dma((4, 2, 2)),
            dma((4, 2, 2, 2)),
            dma((4, 2, 2, 2)),
            dma((4, 2, 3)),
            dma((4, 2, 3)),
            dma((4,)),
            dma((4,)),
        ],
        compiler_params=pltpu.CompilerParams(
            collective_id=0, has_side_effects=True, vmem_limit_bytes=60 * 1024 * 1024
        ),
        name="exchange",
    )(ints, coeffs.T, table, offsets.T, mask.T)
    return result.reshape(CHUNK, 4, MU_DEV)


def solution(mesh):
    return jax.shard_map(
        shards,
        mesh=mesh,
        in_specs=(P("fit", "basis", None), P("fit", "occ"), P("basis", None), P("basis", None)),
        out_specs=P(("fit", "occ"), None, "basis"),
        check_vma=False,
    )
```

```python
import functools

import jax
import jax.numpy as jnp
import numpy as np
from jax import lax
from jax.experimental import pallas as pl
from jax.experimental.pallas import tpu as pltpu
from jax.sharding import PartitionSpec as P

BLK = 64
NNZ = 2
MU_DEV = 128
AUX = 16
ROWS = 3072
CHUNK = 384
QUART = 96
WIDTH = 128
KDIM = AUX * WIDTH
MESH = pl.DeviceIdType.MESH
UNITS = tuple((k, h) for k in range(4) for h in range(2))
X_FIRST = ((0, 0), (1, 0), (2, 0), (3, 0))
N_X = len(X_FIRST)
N_Z = len(UNITS) - N_X
H_ORDER = (0, 1)
SIGN_ENTRIES = (
    (0, 0, 0, 1),
    (0, 1, 1, 1),
    (0, 2, 2, 1),
    (0, 3, 3, 1),
    (1, 0, 1, -1),
    (1, 1, 0, 1),
    (1, 2, 3, -1),
    (1, 3, 2, 1),
    (2, 0, 2, -1),
    (2, 1, 3, 1),
    (2, 2, 0, 1),
    (2, 3, 1, -1),
    (3, 0, 3, -1),
    (3, 1, 2, -1),
    (3, 2, 1, 1),
    (3, 3, 0, 1),
)


def signed_permutations():
    table = np.zeros((WIDTH, 4, WIDTH), np.float32)
    for r, q, s, sign in SIGN_ENTRIES:
        for i in range(WIDTH // 4):
            table[4 * i + q, r, 4 * i + s] = sign
    return table.reshape(WIDTH, 4 * WIDTH)


def dot_nt(a, b):
    return lax.dot_general(
        a, b, (((1,), (1,)), ((), ())), preferred_element_type=jnp.float32
    )


def kernel(
    ints, coef, table, offs, mask, out,
    win_in, ints_v, G, win, mixed, half, part, partf,
    r1a, r1b, r2a, r2b, quarter, fin, last,
    lsem, gs, gr, ws, wr, s1s, s1r, s2s, s2r, qs, qr, ts, tr,
):
    fit = lax.axis_index("fit")
    b = lax.axis_index("basis")
    yl = lax.axis_index("occ")
    z = fit // 4
    x = fit % 4
    yh = b // 2
    c = b % 2
    oyl = 1 - yl
    partner = 2 * yh + (1 - c)

    def basis_at(k):
        return 2 * ((yh + k // 2) % 2) + (c + k % 2) % 2

    def dev(zz, xx, bb, ll):
        return (zz * 4 + xx, bb, ll)

    def rows(q):
        return pl.ds(pl.multiple_of(q * QUART, QUART), QUART)

    locals_ = [pltpu.make_async_copy(ints.at[:, pl.ds(0, MU_DEV), :], win_in, lsem.at[0])]
    for xx in range(4):
        start = pl.multiple_of((2 * xx + yl) * CHUNK, CHUNK)
        locals_.append(
            pltpu.make_async_copy(
                ints.at[:, pl.ds(start, CHUNK), :], ints_v.at[xx], lsem.at[1 + xx]
            )
        )
    for copy in locals_:
        copy.start()

    for t in range(3):
        G[z, x, yl, c, t] = coef[:, pl.ds(pl.multiple_of(c * CHUNK + t * 128, 128), 128)]

    barrier = pltpu.get_barrier_semaphore()

    def greet(target):
        pl.semaphore_signal(barrier, inc=1, device_id=target, device_id_type=MESH)

    for d in (1, 2, 3):
        greet(dev(z, (x + d) % 4, b, yl))
        greet(dev((z + d) % 4, x, b, yl))
    greet(dev(z, x, b, oyl))
    greet(dev(z, x, basis_at(2), oyl))
    greet(dev(z, x, partner, yl))
    pl.semaphore_wait(barrier, 9)

    def send(src, dst, ssem, rsem, target):
        copy = pltpu.make_async_remote_copy(
            src_ref=src,
            dst_ref=dst,
            send_sem=ssem,
            recv_sem=rsem,
            device_id=target,
            device_id_type=MESH,
        )
        copy.start()
        return copy

    sent = []


    near = (1, 3, 2)
    colors = (0, 1)

    def half_piece(color, first, second, o):
        dx, dz = (first, second) if color == 0 else (second, first)
        at = (z + 4 - dz) % 4, (x + 4 - dx) % 4
        return G.at[(*at, o, c)].at[:, pl.ds(32 * color, 32), :]

    def half_group(color, second, o):
        if color == 0:
            return G.at[(z + 4 - second) % 4, :, o, c, :, pl.ds(0, 32), :]
        return G.at[:, (x + 4 - second) % 4, o, c, :, pl.ds(32, 32), :]

    def along(axis, d):
        return dev(z, (x + d) % 4, b, yl) if axis == 0 else dev((z + d) % 4, x, b, yl)

    def gather(phase, color, m, d, ref, target):
        n = m * 4 + d
        copy = send(ref, ref, gs.at[phase, color, n], gr.at[phase, color, n], target)
        sent.append(copy)
        return copy

    one, two, side_y, onchip = {}, {}, {}, []

    def second_stage(color, m):
        for d in near:
            two[color, m, d] = gather(
                1, color, m, d, half_piece(color, m, 0, yl), along(1 - color, d)
            )

    def pair(color, d, o, phase):
        onchip.append(
            gather(phase, color, 0, d, half_group(color, d, o), dev(z, x, partner, yl))
        )

    def outward(color, m, d):
        turn = (yl + color) % 2
        side_y[color, m, d] = gather(
            2, color, m, d, half_piece(color, m, d, yl),
            dev(z, x, 2 * ((yh + turn) % 2) + c, oyl),
        )

    for d in near:
        for color in colors:
            one[color, d] = gather(
                0, color, 0, d, half_piece(color, 0, 0, yl), along(color, d)
            )
    for color in colors:
        second_stage(color, 0)
        outward(color, 0, 0)
    for m in near:
        for color in colors:
            one[color, m].wait_recv()
            second_stage(color, m)
            outward(color, m, 0)
    for m in (0, 1, 3, 2):
        for d in near:
            for color in colors:
                two[color, m, d].wait_recv()
                outward(color, m, d)
    for d in (0, 1, 3, 2):
        for color in colors:
            pair(color, d, yl, 3)
    for d in (0, 1, 3, 2):
        for color in colors:
            for m in (0, 1, 3, 2):
                side_y[color, m, d].wait_recv()
            pair(color, d, oyl, 4)
    for copy in onchip:
        copy.wait_recv()
    zp, zm = (z + 1) % 4, (z + 3) % 4
    xp, xm = (x + 1) % 4, (x + 3) % 4

    lane = lax.broadcasted_iota(jnp.int32, (WIDTH, WIDTH), 1)

    def picked(rb):
        sides = []
        for k in range(NNZ):
            off = offs[k, rb]
            keep = mask[k, rb].astype(jnp.float32)
            odd = lax.rem(off, 2).astype(jnp.float32) * keep
            even = keep - odd
            tile = lax.div(off, 2)
            f = lax.div(tile, 6)
            core = lax.div(lax.rem(tile, 6), 3)
            at = (lax.div(f, 4), lax.rem(f, 4))
            got = jnp.concatenate(
                [G[(*at, o, core, lax.rem(tile, 3))] for o in range(2)], axis=0
            ).astype(jnp.float32)
            turned = pltpu.roll(got, 64, 1)
            if k == 0:
                sides.append(got * even + turned * odd)
            else:
                sides.append(got * odd + turned * even)
        return jnp.where(lane < BLK, sides[0], sides[1]).astype(jnp.bfloat16)

    locals_[0].wait()
    for rb in range(MU_DEV // BLK):
        slab = win_in[:, rb * BLK : (rb + 1) * BLK, :].reshape(AUX * BLK, WIDTH)
        got = dot_nt(slab, picked(rb)).astype(jnp.bfloat16)
        for p in range(AUX):
            win[b, rb * BLK : (rb + 1) * BLK, p * WIDTH : (p + 1) * WIDTH] = got[
                p * BLK : (p + 1) * BLK
            ]
    window = [
        send(win.at[b], win.at[b], ws.at[0], wr.at[0], dev(z, x, partner, yl)),
        send(win.at[b], win.at[b], ws.at[1], wr.at[1], dev(z, x, basis_at(2), oyl)),
    ]
    sent.extend(window)

    for xx in range(4):
        locals_[1 + xx].wait()

    @pl.loop(0, 24, unroll=8)
    def _(i):
        xx = i // 6
        r = i % 6
        slab = ints_v[xx, :, pl.ds(pl.multiple_of(r * BLK, BLK), BLK), :]
        weights = picked((2 * xx + yl) * 6 + r)
        got = dot_nt(slab.reshape(AUX * BLK, WIDTH), weights).astype(jnp.bfloat16)
        at = pl.ds(pl.multiple_of(i * BLK, BLK), BLK)
        for p in range(AUX):
            half[at, p * WIDTH : (p + 1) * WIDTH] = got[p * BLK : (p + 1) * BLK]

    def mix(k, h):
        bb = basis_at(k)

        @pl.loop(0, AUX, unroll=16)
        def _(p):
            at = pl.ds(pl.multiple_of(p * WIDTH, WIDTH), WIDTH)
            signs = table[:, h * 256 : (h + 1) * 256]
            got = jnp.dot(win[bb, :, at], signs, preferred_element_type=jnp.float32)
            got = got.astype(jnp.bfloat16)
            for r in range(2):
                mixed[h, r * 128 : (r + 1) * 128, at] = got[:, r * WIDTH : (r + 1) * WIDTH]

    def dots(k, h):
        @pl.loop(0, 2)
        def _(i):
            at = pl.ds(pl.multiple_of(i * 2 * CHUNK, 2 * CHUNK), 2 * CHUNK)
            got = dot_nt(half[at, :], mixed[h]).reshape(2, CHUNK, 256)
            two = pl.ds(2 * i, 2)
            partf[k, h, two] = got
            part[k, h, two] = got.astype(jnp.bfloat16)

    def color_of(k, h):
        return 0 if (k, h) in X_FIRST else 1

    def slot(k, h):
        same = [u for u in UNITS if color_of(*u) == color_of(k, h)]
        return same.index((k, h))

    def piece(ref, k, h, q, s):
        if color_of(k, h) == 0:
            return ref.at[k, h, q, pl.ds(s * 192, 192)]
        return ref.at[k, h, :, pl.ds(pl.multiple_of(q * QUART + s * 48, 16), 48)]

    def recv_one(k, h, side):
        return (r1a, r1b)[color_of(k, h)].at[slot(k, h), side]

    def recv_two(k, h, side, s):
        return (r2a, r2b)[color_of(k, h)].at[slot(k, h), side, s]

    flights = {}

    def ring(axis):
        if axis == 0:
            return x, lambda d: dev(z, (x + d) % 4, b, yl)
        return z, lambda d: dev((z + d) % 4, x, b, yl)

    def launch(k, h):
        me, peer = ring(color_of(k, h))
        got = {}
        for side in range(2):
            got["one", side] = send(
                piece(part, k, h, (me + 2) % 4, side), recv_one(k, h, side),
                s1s.at[k, h, side], s1r.at[k, h, side], peer(1 + 2 * side),
            )
        for side in range(2):
            got["two", side, 1 - side] = send(
                piece(part, k, h, (me + 1 + 2 * side) % 4, 1 - side),
                recv_two(k, h, side, 1 - side),
                s2s.at[k, h, side, 1 - side], s2r.at[k, h, side, 1 - side],
                peer(1 + 2 * side),
            )
        flights[k, h] = got

    def relay(k, h):
        me, peer = ring(color_of(k, h))
        got = flights[k, h]
        for side in range(2):
            got["one", side].wait_recv()
            at = (me + 1 + 2 * side) % 4
            total = piece(partf, k, h, at, side)[...]
            total += recv_one(k, h, side)[...].astype(jnp.float32)
            piece(part, k, h, at, side)[...] = total.astype(jnp.bfloat16)
            got["two", side, side] = send(
                piece(part, k, h, at, side), recv_two(k, h, side, side),
                s2s.at[k, h, side, side], s2r.at[k, h, side, side], peer(1 + 2 * side),
            )

    def own(ref, k, h, q):
        if color_of(k, h) == 0:
            return ref.at[k, h, x, rows(q)]
        return ref.at[k, h, q, rows(z)]

    def collect(k, h):
        me, _ = ring(color_of(k, h))
        got = flights[k, h]
        for s in range(2):
            got["two", 0, s].wait_recv()
            got["two", 1, s].wait_recv()
            total = piece(partf, k, h, me, s)[...]
            total += recv_two(k, h, 0, s)[...].astype(jnp.float32)
            total += recv_two(k, h, 1, s)[...].astype(jnp.float32)
            piece(partf, k, h, me, s)[...] = total
            piece(part, k, h, me, s)[...] = total.astype(jnp.bfloat16)
        me, peer = ring(1 - color_of(k, h))
        for d in (2, 1, 3):
            got["far", d] = send(
                own(part, k, h, (me + d) % 4), quarter.at[k, h, d - 1],
                qs.at[k, h, d - 1], qr.at[k, h, d - 1], peer(d),
            )

    def finish(k, h):
        me, _ = ring(1 - color_of(k, h))
        got = flights[k, h]
        total = own(partf, k, h, me)[...]
        for d in (1, 3, 2):
            got["far", d].wait_recv()
            total += quarter[k, h, d - 1].astype(jnp.float32)
        fin[k, :, h * 256 : (h + 1) * 256] = total.astype(jnp.bfloat16)

    finals = []

    def deliver(k):
        target = dev(b, x, basis_at(k), yl)
        if k == 0:
            same = z == b

            @pl.when(same)
            def _():
                pltpu.make_async_copy(fin.at[k], last.at[z], tr.at[z]).start()

            @pl.when(jnp.logical_not(same))
            def _():
                send(fin.at[k], last.at[z], ts.at[k], tr.at[z], target)
        else:
            finals.append(send(fin.at[k], last.at[z], ts.at[k], tr.at[z], target))

    order = (0, 1, 2, 3)
    forward = None
    for i, k in enumerate(order):
        if k == 2:
            window[1].wait_recv()
            other = win.at[basis_at(2)]
            forward = send(other, other, ws.at[2], wr.at[2], dev(z, x, partner, yl))
            sent.append(forward)
        elif k == 3:
            forward.wait_recv()
        elif k == 1:
            window[0].wait_recv()
        for h in H_ORDER:
            mix(k, h)
            dots(k, h)
            if i >= 1:
                relay(order[i - 1], h)
            launch(k, h)
            if i >= 2:
                collect(order[i - 2], h)
    for h in range(2):
        relay(order[3], h)
    for h in range(2):
        collect(order[2], h)
    for h in range(2):
        collect(order[3], h)
    for i in range(4):
        for h in range(2):
            finish(order[i], h)
        deliver(order[i])

    for q in range(4):
        pltpu.make_async_copy(fin.at[0], last.at[q], tr.at[q]).wait()
        for r in range(4):
            out[pl.ds(q * CHUNK + r, QUART, stride=4), :] = last[
                q, :, r * MU_DEV : (r + 1) * MU_DEV
            ].astype(jnp.float32)
    for copy in sent:
        copy.wait_send()
    for got in flights.values():
        for copy in got.values():
            copy.wait_send()

    @pl.when(z != b)
    def _():
        pltpu.make_async_remote_copy(
            src_ref=fin.at[0], dst_ref=last.at[z], send_sem=ts.at[0], recv_sem=tr.at[z],
            device_id=dev(b, x, b, yl), device_id_type=MESH,
        ).wait_send()

    for copy in finals:
        copy.wait_send()


def shards(ints, coeffs, offsets, mask):
    table = jnp.asarray(signed_permutations(), jnp.bfloat16)
    bf16, f32 = jnp.bfloat16, jnp.float32
    vmem = pl.BlockSpec(memory_space=pltpu.VMEM)
    smem = pl.BlockSpec(memory_space=pltpu.SMEM)
    dma = pltpu.SemaphoreType.DMA
    result = pl.pallas_call(
        kernel,
        out_shape=jax.ShapeDtypeStruct((4 * CHUNK, MU_DEV), f32),
        in_specs=[pl.BlockSpec(memory_space=pl.ANY), vmem, vmem, smem, smem],
        out_specs=vmem,
        scratch_shapes=[
            pltpu.VMEM((AUX, MU_DEV, WIDTH), bf16),
            pltpu.VMEM((4, AUX, CHUNK, WIDTH), bf16),
            pltpu.VMEM((4, 4, 2, 2, 3, 64, 128), bf16),
            pltpu.VMEM((4, MU_DEV, KDIM), bf16),
            pltpu.VMEM((2, 256, KDIM), bf16),
            pltpu.VMEM((4 * CHUNK, KDIM), bf16),
            pltpu.VMEM((4, 2, 4, CHUNK, 256), bf16),
            pltpu.VMEM((4, 2, 4, CHUNK, 256), f32),
            pltpu.VMEM((N_X, 2, 192, 256), bf16),
            pltpu.VMEM((N_Z, 2, 4, 48, 256), bf16),
            pltpu.VMEM((N_X, 2, 2, 192, 256), bf16),
            pltpu.VMEM((N_Z, 2, 2, 4, 48, 256), bf16),
            pltpu.VMEM((4, 2, 3, QUART, 256), bf16),
            pltpu.VMEM((4, QUART, 512), bf16),
            pltpu.VMEM((4, QUART, 512), bf16),
            dma((5,)),
            dma((5, 2, 16)),
            dma((5, 2, 16)),
            dma((3,)),
            dma((3,)),
            dma((4, 2, 2)),
            dma((4, 2, 2)),
            dma((4, 2, 2, 2)),
            dma((4, 2, 2, 2)),
            dma((4, 2, 3)),
            dma((4, 2, 3)),
            dma((4,)),
            dma((4,)),
        ],
        compiler_params=pltpu.CompilerParams(
            collective_id=0, has_side_effects=True, vmem_limit_bytes=60 * 1024 * 1024
        ),
        name="exchange",
    )(ints, coeffs.T, table, offsets.T, mask.T)
    return result.reshape(CHUNK, 4, MU_DEV)


def solution(mesh):
    return jax.shard_map(
        shards,
        mesh=mesh,
        in_specs=(P("fit", "basis", None), P("fit", "occ"), P("basis", None), P("basis", None)),
        out_specs=P(("fit", "occ"), None, "basis"),
        check_vma=False,
    )
```
